32 devices in a mesh: rep: 2 (over y), slab: 16 (over z, x, core).
Axes of the slice: x: 2, y: 2, z: 4, core: 2. Of those that a mesh axis runs over, the one named last changes fastest.
Arguments:
- spins: float32 [8, 3, 128, 16, 256], P('rep', None, 'slab'), as said below
- couplings: int32 [3, 128, 16, 256], P(None, 'slab'), may hold values from 0 to 1
- source: int32 [8], replicated, may hold values from 0 to 7, as said below
Outputs:
- annealed: float32 [8, 3, 128, 16, 256], P('rep', None, 'slab')
The draws below stay inside these ranges and needn't reach their ends.
Inputs may be any that keep to these rules, and one draw needn't show every extreme that they name: Slot d = g * 4 + l (rep group g, local index l) either copies its own replica (source[d] = d) or copies a replica of group (g + 1 + l // 2) mod 2 whose own slot copies itself. In every group at least one of slots 0 and 1 and at least one of slots 2 and 3 copy in this way. Some group has two slots that copy replicas of one other group. `spins`: each replica is a unit vector at every site.
All inputs are finite; a program needn't handle non-finite values.
Results may differ from the reference program's by a relative error of at most 0.0003.
Values sent between devices are 32-bit elements; how exact they have to be, the bound alone decides.
A program may use at most 64 MiB of HBM per device.

```python
import jax
import jax.numpy as jnp
from jax import lax

NX = 256
NY = 16
REP_DEV = 4
SWEEPS = 4
NZ = 128
REPLICAS = 8
N_REP = 2


def draw_spins(key, part):
    raw = jax.random.normal(key, (REPLICAS, 3, NZ, NY, NX), jnp.float32)
    length = jnp.sqrt(jnp.sum(raw * raw, axis=1, keepdims=True))
    return raw / jnp.maximum(length, 0.001)


def draw_source(key, part):
    key_keep, key_group, key_bits, key_pick, key_low = jax.random.split(jax.random.fold_in(key, 7), 5)
    groups = jnp.arange(N_REP, dtype=jnp.int32)
    local = jnp.arange(REP_DEV, dtype=jnp.int32)
    keep_slot = 2 + jax.random.randint(key_keep, (N_REP,), 0, REP_DEV - 2)
    low_slot = jax.random.randint(key_low, (N_REP,), 0, 2)
    first_group = jax.random.randint(key_group, (), 0, N_REP)
    bits = jax.random.randint(key_bits, (N_REP, REP_DEV), 0, 2)
    forced = (groups[:, None] == first_group) & (local[None, :] < 2)
    forced = forced | (local[None, :] == low_slot[:, None]) | (local[None, :] == (5 - keep_slot)[:, None])
    survive = local[None, :] == keep_slot[:, None]
    killed = ((bits == 1) | forced) & jnp.logical_not(survive)
    scores = jax.random.randint(key_pick, (N_REP, REP_DEV), 0, 1 << 20) * REP_DEV + local[None, :]
    masked = jnp.where(killed, -1, scores)
    picked = jnp.argmax(masked, axis=1).astype(jnp.int32)
    giver = (groups[:, None] + 1 + local[None, :] // 2) % N_REP
    anchor = giver * REP_DEV + jnp.take(picked, giver)
    own = groups[:, None] * REP_DEV + local[None, :]
    return jnp.where(killed, anchor, own).reshape(-1).astype(jnp.int32)


def touch_ends(drawn, key, smallest, largest):
    dims = drawn.shape
    place = [jax.random.randint(jax.random.fold_in(key, axis), (), 0, dims[axis]) for axis in range(len(dims))]
    drawn = drawn.at[tuple(place)].set(smallest)
    longest = dims.index(max(dims))
    place[longest] = (place[longest] + 1) % dims[longest]
    return drawn.at[tuple(place)].set(largest)


def setup_inputs(seed: int = 0) -> dict:
    arg_keys = jax.random.split(jax.random.key(seed), 4)
    spins = draw_spins(jax.random.fold_in(arg_keys[3], 71), 0)
    couplings = touch_ends(jax.random.randint(arg_keys[1], (3, NZ, NY, NX), 0, 2), jax.random.fold_in(arg_keys[1], 1), 0, 1).astype(jnp.int32)
    source = draw_source(jax.random.fold_in(arg_keys[3], 71), 0)
    return dict(spins=spins, couplings=couplings, source=source)


def field_ref(lattice, bonds):
    east = bonds[0] * jnp.roll(lattice, -1, axis=3)
    west = jnp.roll(bonds[0] * lattice, 1, axis=3)
    north = bonds[1] * jnp.roll(lattice, -1, axis=2)
    south = jnp.roll(bonds[1] * lattice, 1, axis=2)
    upper = bonds[2] * jnp.roll(lattice, -1, axis=1)
    lower = jnp.roll(bonds[2] * lattice, 1, axis=1)
    return ((((east + west) + north) + south) + upper) + lower


def relax_ref(lattice, local_field, mask):
    along = jnp.sum(lattice * local_field, axis=0, keepdims=True)
    strength = jnp.sum(local_field * local_field, axis=0, keepdims=True)
    turned = 2.0 * along / jnp.maximum(strength, 1.0) * local_field - lattice
    return jnp.where(mask, turned, lattice)


def reference(spins, couplings, source):
    bonds = (2 * couplings - 1).astype(jnp.float32)
    copied = jnp.take(spins, source.astype(jnp.int32), axis=0)
    shape = (NZ, NY, NX)
    total = lax.broadcasted_iota(jnp.int32, shape, 0) + lax.broadcasted_iota(jnp.int32, shape, 1) + lax.broadcasted_iota(jnp.int32, shape, 2)
    masks = [((total % 2) == colour)[None] for colour in range(2)]

    def one_replica(lattice):
        for sweep in range(SWEEPS):
            for colour in range(2):
                local_field = field_ref(lattice, bonds)
                lattice = relax_ref(lattice, local_field, masks[colour])
        return lattice

    return lax.map(one_replica, copied)
```

```python
import functools

import jax
import jax.numpy as jnp
from jax import lax
from jax.experimental import pallas as pl
from jax.experimental.pallas import tpu as pltpu
from jax.sharding import PartitionSpec as P

SWEEPS = 4
WIDTH = 2
MESH = pl.DeviceIdType.MESH


def reverse_rows(value, row):
    count = value.shape[0]
    shift = 1
    while shift < count:
        down = pltpu.roll(value, shift, 0)
        if 2 * shift == count:
            value = down
        else:
            value = jnp.where((row & shift) == 0, pltpu.roll(value, count - shift, 0), down)
        shift *= 2
    return value


def halo_items(width, colour):
    below = [(0, 1 - colour)] + [(d, c) for d in range(1, width) for c in range(2)]
    above = [(d, c) for d in range(width - 1) for c in range(2)] + [(width - 1, 1 - colour)]
    return below, above


def kernel(n_rep, n_slab, source, spins, coup, out, work, bonds, low, high, stage, land, res, c_send, c_recv, h_send, h_recv, r_send, r_recv):
    rep_dev, comps, planes, rows, cols = spins.shape
    pairs = rep_dev // 2
    width, half = WIDTH, rows // 2
    exchanges = 2 * SWEEPS // width
    group, slab = lax.axis_index("rep"), lax.axis_index("slab")
    up, down = lax.rem(slab + 1, n_slab), lax.rem(slab + n_slab - 1, n_slab)
    offsets = [(1 + j) % n_rep for j in range(pairs)]
    remote = [j for j in range(pairs) if offsets[j]]

    barrier = pltpu.get_barrier_semaphore()
    for side in (up, down):
        pl.semaphore_signal(barrier, inc=1, device_id=(group, side), device_id_type=MESH)
    for j in remote:
        giver = lax.rem(group + offsets[j], n_rep)
        pl.semaphore_signal(barrier, inc=1, device_id=(giver, slab), device_id_type=MESH)
    pl.semaphore_wait(barrier, 2 + len(remote))

    def remote_copy(src, dst, send, recv, device):
        copy = pltpu.make_async_remote_copy(
            src_ref=src, dst_ref=dst, send_sem=send, recv_sem=recv, device_id=device, device_id_type=MESH
        )
        copy.start()
        return copy

    bond_copies = [remote_copy(coup.at[2, planes - width], low.at[2, 0], c_send.at[0], c_recv.at[0], (group, up))]
    if width > 1:
        bond_copies.append(
            remote_copy(coup.at[:, planes - width + 1 : planes], low.at[:, 1:width], c_send.at[1], c_recv.at[1], (group, up))
        )
        bond_copies.append(remote_copy(coup.at[:, 0 : width - 1], high, c_send.at[2], c_recv.at[2], (group, down)))

    row = lax.broadcasted_iota(jnp.int32, (half, cols), 0)
    site = row + lax.broadcasted_iota(jnp.int32, (half, cols), 1)

    def front(plane):
        return ((site + (slab * planes + plane + width)) & 1) == 0

    def pack(mask, first, second):
        second = reverse_rows(second, row)
        return jnp.where(mask, first, second), jnp.where(mask, second, first)

    copies = {}

    def send_halo(r, e):
        colour = (e * width) % 2
        below, above = halo_items(width, colour)
        for side, (items, start, device) in enumerate(((below, planes, up), (above, width, down))):
            for i, (d, c) in enumerate(items):
                for k in range(comps):
                    stage[e, side, r, i, k] = work[r, start + d, c, k]
            copies[r, e, side] = remote_copy(
                stage.at[e, side, r], land.at[e, side, r], h_send.at[e, side, r], h_recv.at[e, side, r], (group, device)
            )

    def take_halo(r, e):
        colour = (e * width) % 2
        below, above = halo_items(width, colour)
        for side, (items, start) in enumerate(((below, 0), (above, planes + width))):
            copies[r, e, side].wait()
            for i, (d, c) in enumerate(items):
                for k in range(comps):
                    work[r, start + d, c, k] = land[e, side, r, i, k]

    kept = []
    for slot in range(rep_dev):
        own = group * rep_dev + slot
        kept.append(source[own] == own)

    for r in range(pairs):

        def pack_plane(p, carry, r=r):
            mask = front(p + width)
            for k in range(comps):
                value = jnp.where(kept[2 * r], spins[2 * r, k, p], spins[2 * r + 1, k, p])
                zero, one = pack(mask, value[:half], value[half:])
                work[r, p + width, 0, k] = zero
                work[r, p + width, 1, k] = one
            return carry

        lax.fori_loop(0, planes, pack_plane, 0)
        send_halo(r, 0)

    def bonds_of(plane, jx, jy, jz, jz_below):
        mask = front(plane)
        jx, jy, jz, jz_below = [(2 * j - 1).astype(jnp.float32) for j in (jx, jy, jz, jz_below)]
        jw = pltpu.roll(jx, 1, 1)
        first, second = jy[:half], jy[half:]
        south_first = jnp.where(row == 0, second[half - 1 :], pltpu.roll(first, 1, 0))
        south_second = jnp.where(row == 0, first[half - 1 :], pltpu.roll(second, 1, 0))
        first_r = reverse_rows(second, row)
        south_r = reverse_rows(south_second, row)
        east = pack(mask, jx[:half], jx[half:])
        west = pack(mask, jw[:half], jw[half:])
        upper = pack(mask, jz[:half], jz[half:])
        lower = pack(mask, jz_below[:half], jz_below[half:])
        after = (jnp.where(mask, first, south_r), jnp.where(mask, south_r, first))
        before = (jnp.where(mask, south_first, first_r), jnp.where(mask, first_r, south_first))
        for i, bond in enumerate((east, west, after, before, upper, lower)):
            for c in range(2):
                bonds[plane, c, i] = bond[c]

    def own_bonds(p, carry):
        bonds_of(p + width, coup[0, p], coup[1, p], coup[2, p], coup[2, p - 1])
        return carry

    lax.fori_loop(1, planes, own_bonds, 0)
    for copy in bond_copies:
        copy.wait()
    for p in range(1, width):
        bonds_of(p, low[0, p], low[1, p], low[2, p], low[2, p - 1])
    bonds_of(width, coup[0, 0], coup[1, 0], coup[2, 0], low[2, width - 1])
    for p in range(width - 1):
        beneath = coup[2, planes - 1] if p == 0 else high[2, p - 1]
        bonds_of(planes + width + p, high[0, p], high[1, p], high[2, p], beneath)

    def half_sweep(r, colour, first, last):
        other = 1 - colour

        def one_plane(p, carry):
            east, west, after, before, upper, lower = [bonds[p, colour, i] for i in range(6)]
            field, spin = [], []
            for k in range(comps):
                q = work[r, p, other, k]
                north = jnp.where(row == half - 1, q, pltpu.roll(q, half - 1, 0))
                south = jnp.where(row == 0, q, pltpu.roll(q, 1, 0))
                h = east * pltpu.roll(q, cols - 1, 1) + west * pltpu.roll(q, 1, 1)
                h = h + after * north + before * south
                h = h + upper * work[r, p + 1, other, k] + lower * work[r, p - 1, other, k]
                field.append(h)
                spin.append(work[r, p, colour, k])
            along = sum(s * h for s, h in zip(spin, field))
            strength = sum(h * h for h in field)
            scale = 2.0 * along / jnp.maximum(strength, 1.0)
            for k in range(comps):
                work[r, p, colour, k] = scale * field[k] - spin[k]
            return carry

        lax.fori_loop(first, last, one_plane, 0)

    results = []
    for e in range(exchanges):
        for r in range(pairs):
            take_halo(r, e)
            for i in range(width):
                half_sweep(r, (e * width + i) % 2, i + 1, planes + 2 * width - 1 - i)
            if e < exchanges - 1:
                send_halo(r, e + 1)
            else:
                for n, j in enumerate(remote):
                    taker = lax.rem(group + n_rep - offsets[j], n_rep)
                    results.append(
                        remote_copy(
                            work.at[r, width : width + planes], res.at[n, r], r_send.at[n, r], r_recv.at[n, r], (taker, slab)
                        )
                    )

    def write(j):
        if j in remote:
            n = remote.index(j)
            given = lambda r, p, c, k: res[n, r, p, c, k]
        else:
            given = lambda r, p, c, k: work[r, p + width, c, k]

        def write_plane(p, carry):
            mask = front(p + width)
            for slot in (2 * j, 2 * j + 1):
                pair = lax.rem(source[group * rep_dev + slot], rep_dev) // 2
                for k in range(comps):
                    colours = []
                    for c in range(2):
                        value = given(0, p, c, k)
                        for r in range(1, pairs):
                            value = jnp.where(pair == r, given(r, p, c, k), value)
                        colours.append(jnp.where(kept[slot], work[j, p + width, c, k], value))
                    zero, one = colours
                    out[slot, k, p, :half] = jnp.where(mask, zero, one)
                    out[slot, k, p, half:] = reverse_rows(jnp.where(mask, one, zero), row)
            return carry

        lax.fori_loop(0, planes, write_plane, 0)

    for j in range(pairs):
        if j not in remote:
            write(j)
    for copy in results:
        copy.wait()
    for j in remote:
        write(j)


def solution(mesh):
    n_rep, n_slab = mesh.shape["rep"], mesh.shape["slab"]

    def local(spins, couplings, source):
        rep_dev, comps, planes, rows, cols = spins.shape
        pairs, half, width = rep_dev // 2, rows // 2, WIDTH
        exchanges, items = 2 * SWEEPS // width, 2 * width - 1
        n_remote = sum(1 for j in range(pairs) if (1 + j) % n_rep)
        deep = planes + 2 * width
        f32, i32, dma = jnp.float32, jnp.int32, pltpu.SemaphoreType.DMA
        return pl.pallas_call(
            functools.partial(kernel, n_rep, n_slab),
            out_shape=jax.ShapeDtypeStruct(spins.shape, f32),
            in_specs=[
                pl.BlockSpec(memory_space=pltpu.SMEM),
                pl.BlockSpec(memory_space=pltpu.VMEM),
                pl.BlockSpec(memory_space=pltpu.VMEM),
            ],
            out_specs=pl.BlockSpec(memory_space=pltpu.VMEM),
            scratch_shapes=[
                pltpu.VMEM((pairs, deep, 2, comps, half, cols), f32),
                pltpu.VMEM((deep, 2, 6, half, cols), f32),
                pltpu.VMEM((3, width, rows, cols), i32),
                pltpu.VMEM((3, max(width - 1, 1), rows, cols), i32),
                pltpu.VMEM((exchanges, 2, pairs, items, comps, half, cols), f32),
                pltpu.VMEM((exchanges, 2, pairs, items, comps, half, cols), f32),
                pltpu.VMEM((max(n_remote, 1), pairs, planes, 2, comps, half, cols), f32),
                dma((3,)),
                dma((3,)),
                dma((exchanges, 2, pairs)),
                dma((exchanges, 2, pairs)),
                dma((max(n_remote, 1), pairs)),
                dma((max(n_remote, 1), pairs)),
            ],
            compiler_params=pltpu.CompilerParams(collective_id=0, has_side_effects=True),
        )(source, spins, couplings)

    in_specs = (P("rep", None, "slab", None, None), P(None, "slab", None, None), P())
    out_specs = P("rep", None, "slab", None, None)
    return jax.shard_map(local, mesh=mesh, in_specs=in_specs, out_specs=out_specs, check_vma=False)
```

```python
import functools

import jax
import jax.numpy as jnp
from jax import lax
from jax.experimental import pallas as pl
from jax.experimental.pallas import tpu as pltpu
from jax.sharding import PartitionSpec as P

SWEEPS = 4
GROUP = 5
WIDTH = 2
MESH = pl.DeviceIdType.MESH


def reverse_rows(value, row):
    count = value.shape[0]
    shift = 1
    while shift < count:
        down = pltpu.roll(value, shift, 0)
        if 2 * shift == count:
            value = down
        else:
            value = jnp.where((row & shift) == 0, pltpu.roll(value, count - shift, 0), down)
        shift *= 2
    return value


def halo_items(width, colour):
    below = [(0, 1 - colour)] + [(d, c) for d in range(1, width) for c in range(2)]
    above = [(d, c) for d in range(width - 1) for c in range(2)] + [(width - 1, 1 - colour)]
    return below, above


def kernel(n_rep, n_slab, source, spins_hbm, coup_hbm, out_hbm, spins, coup, out, raw, work, bonds, low, high, stage, land, res, c_send, c_recv, h_send, h_recv, r_send, r_recv, in_sem, out_sem):
    rep_dev, comps, planes, rows, cols = spins.shape
    pairs = rep_dev // 2
    width, half = WIDTH, rows // 2
    exchanges = 2 * SWEEPS // width
    group, slab = lax.axis_index("rep"), lax.axis_index("slab")
    up, down = lax.rem(slab + 1, n_slab), lax.rem(slab + n_slab - 1, n_slab)
    offsets = [(1 + j) % n_rep for j in range(pairs)]
    remote = [j for j in range(pairs) if offsets[j]]

    loads = [pltpu.make_async_copy(spins_hbm.at[pl.ds(2 * r, 2)], spins.at[pl.ds(2 * r, 2)], in_sem.at[r]) for r in range(pairs)]
    loads.append(pltpu.make_async_copy(coup_hbm, coup, in_sem.at[pairs]))
    for copy in loads:
        copy.start()

    barrier = pltpu.get_barrier_semaphore()
    for side in (up, down):
        pl.semaphore_signal(barrier, inc=1, device_id=(group, side), device_id_type=MESH)
    for j in remote:
        giver = lax.rem(group + offsets[j], n_rep)
        pl.semaphore_signal(barrier, inc=1, device_id=(giver, slab), device_id_type=MESH)
    def remote_copy(src, dst, send, recv, device):
        copy = pltpu.make_async_remote_copy(
            src_ref=src, dst_ref=dst, send_sem=send, recv_sem=recv, device_id=device, device_id_type=MESH
        )
        copy.start()
        return copy

    row = lax.broadcasted_iota(jnp.int32, (half, cols), 0)
    site = row + lax.broadcasted_iota(jnp.int32, (half, cols), 1)

    def front(plane):
        return ((site + (slab * planes + plane + width)) & 1) == 0

    def pack(mask, first, second):
        second = reverse_rows(second, row)
        return jnp.where(mask, first, second), jnp.where(mask, second, first)

    copies = {}

    def send_halo(r, e):
        colour = (e * width) % 2
        below, above = halo_items(width, colour)
        for side, (items, start, device) in enumerate(((below, planes, up), (above, width, down))):
            for i, (d, c) in enumerate(items):
                for k in range(comps):
                    stage[e, side, r, i, k] = work[r, start + d, c, k]
            copies[r, e, side] = remote_copy(
                stage.at[e, side, r], land.at[e, side, r], h_send.at[e, side, r], h_recv.at[e, side, r], (group, device)
            )

    def take_halo(r, e):
        colour = (e * width) % 2
        below, above = halo_items(width, colour)
        for side, (items, start) in enumerate(((below, 0), (above, planes + width))):
            copies[r, e, side].wait()
            for i, (d, c) in enumerate(items):
                for k in range(comps):
                    work[r, start + d, c, k] = land[e, side, r, i, k]

    kept = []
    for slot in range(rep_dev):
        own = group * rep_dev + slot
        kept.append(source[own] == own)

    for r in range(pairs):
        loads[r].wait()

        def pack_plane(p, carry, r=r):
            mask = front(p + width)
            for k in range(comps):
                value = jnp.where(kept[2 * r], spins[2 * r, k, p], spins[2 * r + 1, k, p])
                zero, one = pack(mask, value[:half], value[half:])
                work[r, p + width, 0, k] = zero
                work[r, p + width, 1, k] = one
                if r == 0 and remote:
                    raw[p, 0, k] = zero
                    raw[p, 1, k] = one
            return carry

        lax.fori_loop(0, planes, pack_plane, 0)

    def bonds_of(plane, jx, jy, jz, jz_below):
        mask = front(plane)
        jx, jy, jz, jz_below = [(2 * j - 1).astype(jnp.float32) for j in (jx, jy, jz, jz_below)]
        jw = pltpu.roll(jx, 1, 1)
        first, second = jy[:half], jy[half:]
        south_first = jnp.where(row == 0, second[half - 1 :], pltpu.roll(first, 1, 0))
        south_second = jnp.where(row == 0, first[half - 1 :], pltpu.roll(second, 1, 0))
        first_r = reverse_rows(second, row)
        south_r = reverse_rows(south_second, row)
        east = pack(mask, jx[:half], jx[half:])
        west = pack(mask, jw[:half], jw[half:])
        upper = pack(mask, jz[:half], jz[half:])
        lower = pack(mask, jz_below[:half], jz_below[half:])
        after = (jnp.where(mask, first, south_r), jnp.where(mask, south_r, first))
        before = (jnp.where(mask, south_first, first_r), jnp.where(mask, first_r, south_first))
        for i, bond in enumerate((east, west, after, before, upper, lower)):
            for c in range(2):
                bonds[plane, c, i] = bond[c]

    def own_bonds(p, carry):
        bonds_of(p + width, coup[0, p], coup[1, p], coup[2, p], coup[2, p - 1])
        return carry

    loads[pairs].wait()
    lax.fori_loop(1, planes, own_bonds, 0)
    pl.semaphore_wait(barrier, 2 + len(remote))

    bond_copies = [remote_copy(coup.at[2, planes - width], low.at[2, 0], c_send.at[0], c_recv.at[0], (group, up))]
    if width > 1:
        bond_copies.append(
            remote_copy(coup.at[:, planes - width + 1 : planes], low.at[:, 1:width], c_send.at[1], c_recv.at[1], (group, up))
        )
        bond_copies.append(remote_copy(coup.at[:, 0 : width - 1], high, c_send.at[2], c_recv.at[2], (group, down)))
    inner = pl.ds(width, planes)
    results, late = [], []
    for n, j in enumerate(remote):
        taker = lax.rem(group + n_rep - offsets[j], n_rep)
        late.append(remote_copy(raw, work.at[pairs + n, inner], r_send.at[n, 0], r_recv.at[n, 0], (taker, slab)))
    for r in range(pairs - 1, -1, -1):
        send_halo(r, 0)
    for copy in bond_copies:
        copy.wait()
    for p in range(1, width):
        bonds_of(p, low[0, p], low[1, p], low[2, p], low[2, p - 1])
    bonds_of(width, coup[0, 0], coup[1, 0], coup[2, 0], low[2, width - 1])
    for p in range(width - 1):
        beneath = coup[2, planes - 1] if p == 0 else high[2, p - 1]
        bonds_of(planes + width + p, high[0, p], high[1, p], high[2, p], beneath)

    def half_sweep(r, colour, first, last):
        other = 1 - colour

        def turned(p):
            east, west, after, before, upper, lower = [bonds[p, colour, i] for i in range(6)]
            field, spin = [], []
            for k in range(comps):
                q = work[r, p, other, k]
                north = jnp.where(row == half - 1, q, pltpu.roll(q, half - 1, 0))
                south = jnp.where(row == 0, q, pltpu.roll(q, 1, 0))
                h = east * pltpu.roll(q, cols - 1, 1) + west * pltpu.roll(q, 1, 1)
                h = h + after * north + before * south
                h = h + upper * work[r, p + 1, other, k] + lower * work[r, p - 1, other, k]
                field.append(h)
                spin.append(work[r, p, colour, k])
            along = sum(s * h for s, h in zip(spin, field))
            strength = sum(h * h for h in field)
            scale = 2.0 * along / jnp.maximum(strength, 1.0)
            return [scale * h - s for s, h in zip(spin, field)]

        count = last - first
        step = max(g for g in range(1, GROUP + 1) if count % g == 0)

        def some_planes(i, carry):
            base = first + i * step
            new = [turned(base + n) for n in range(step)]
            for n in range(step):
                for k in range(comps):
                    work[r, base + n, colour, k] = new[n][k]
            return carry

        lax.fori_loop(0, count // step, some_planes, 0)

    def advance(r, e):
        take_halo(r, e)
        for i in range(width):
            half_sweep(r, (e * width + i) % 2, i + 1, planes + 2 * width - 1 - i)
        if e < exchanges - 1:
            send_halo(r, e + 1)
        elif 1 <= r < pairs:
            for n, j in enumerate(remote):
                taker = lax.rem(group + n_rep - offsets[j], n_rep)
                results.append(
                    remote_copy(work.at[r, inner], res.at[n, r - 1], r_send.at[n, r], r_recv.at[n, r], (taker, slab))
                )

    for e in range(exchanges):
        for r in range(pairs - 1, -1, -1):
            advance(r, e)
        if e == 0:
            for n, copy in enumerate(late):
                copy.wait_recv()
                send_halo(pairs + n, 0)
        elif e < exchanges - 1:
            for n in range(len(late)):
                advance(pairs + n, e - 1)

    def write(j):
        if j in remote:
            n = remote.index(j)
            given = lambda r, p, c, k: res[n, r - 1, p, c, k] if r else work[pairs + n, p + width, c, k]
        else:
            given = lambda r, p, c, k: work[r, p + width, c, k]

        def write_plane(p, carry):
            mask = front(p + width)
            for slot in (2 * j, 2 * j + 1):
                pair = lax.rem(source[group * rep_dev + slot], rep_dev) // 2
                for k in range(comps):
                    colours = []
                    for c in range(2):
                        value = given(0, p, c, k)
                        for r in range(1, pairs):
                            value = jnp.where(pair == r, given(r, p, c, k), value)
                        colours.append(jnp.where(kept[slot], work[j, p + width, c, k], value))
                    zero, one = colours
                    out[slot, k, p, :half] = jnp.where(mask, zero, one)
                    out[slot, k, p, half:] = reverse_rows(jnp.where(mask, one, zero), row)
            return carry

        lax.fori_loop(0, planes, write_plane, 0)

    stores = []

    def store(j):
        write(j)
        stores.append(pltpu.make_async_copy(out.at[pl.ds(2 * j, 2)], out_hbm.at[pl.ds(2 * j, 2)], out_sem.at[j]))
        stores[-1].start()

    for j in range(pairs):
        if j not in remote:
            store(j)
    for e in range(max(exchanges - 2, 0), exchanges):
        for n in range(len(late)):
            advance(pairs + n, e)
    for copy in late:
        copy.wait_send()
    for copy in results:
        copy.wait()
    for j in remote:
        store(j)
    for copy in stores:
        copy.wait()


def solution(mesh):
    n_rep, n_slab = mesh.shape["rep"], mesh.shape["slab"]

    def local(spins, couplings, source):
        rep_dev, comps, planes, rows, cols = spins.shape
        pairs, half, width = rep_dev // 2, rows // 2, WIDTH
        exchanges, items = 2 * SWEEPS // width, 2 * width - 1
        n_remote = sum(1 for j in range(pairs) if (1 + j) % n_rep)
        deep = planes + 2 * width
        f32, i32, dma = jnp.float32, jnp.int32, pltpu.SemaphoreType.DMA
        return pl.pallas_call(
            functools.partial(kernel, n_rep, n_slab),
            out_shape=jax.ShapeDtypeStruct(spins.shape, f32),
            in_specs=[
                pl.BlockSpec(memory_space=pltpu.SMEM),
                pl.BlockSpec(memory_space=pl.ANY),
                pl.BlockSpec(memory_space=pl.ANY),
            ],
            out_specs=pl.BlockSpec(memory_space=pl.ANY),
            scratch_shapes=[
                pltpu.VMEM(spins.shape, f32),
                pltpu.VMEM(couplings.shape, i32),
                pltpu.VMEM(spins.shape, f32),
                pltpu.VMEM((planes, 2, comps, half, cols), f32),
                pltpu.VMEM((pairs + n_remote, deep, 2, comps, half, cols), f32),
                pltpu.VMEM((deep, 2, 6, half, cols), f32),
                pltpu.VMEM((3, width, rows, cols), i32),
                pltpu.VMEM((3, max(width - 1, 1), rows, cols), i32),
                pltpu.VMEM((exchanges, 2, pairs + n_remote, items, comps, half, cols), f32),
                pltpu.VMEM((exchanges, 2, pairs + n_remote, items, comps, half, cols), f32),
                pltpu.VMEM((max(n_remote, 1), pairs - 1, planes, 2, comps, half, cols), f32),
                dma((3,)),
                dma((3,)),
                dma((exchanges, 2, pairs + n_remote)),
                dma((exchanges, 2, pairs + n_remote)),
                dma((max(n_remote, 1), pairs)),
                dma((max(n_remote, 1), pairs)),
                dma((pairs + 1,)),
                dma((pairs,)),
            ],
            compiler_params=pltpu.CompilerParams(collective_id=0, has_side_effects=True),
        )(source, spins, couplings)

    in_specs = (P("rep", None, "slab", None, None), P(None, "slab", None, None), P())
    out_specs = P("rep", None, "slab", None, None)
    return jax.shard_map(local, mesh=mesh, in_specs=in_specs, out_specs=out_specs, check_vma=False)
```

```python
import functools

import jax
import jax.numpy as jnp
from jax import lax
from jax.experimental import pallas as pl
from jax.experimental.pallas import tpu as pltpu
from jax.sharding import PartitionSpec as P

SWEEPS = 4
GROUP = 5
WIDTH = 2
MESH = pl.DeviceIdType.MESH


def reverse_rows(value, row):
    count = value.shape[0]
    shift = 1
    while shift < count:
        down = pltpu.roll(value, shift, 0)
        if 2 * shift == count:
            value = down
        else:
            value = jnp.where((row & shift) == 0, pltpu.roll(value, count - shift, 0), down)
        shift *= 2
    return value


def halo_items(width, colour, first):
    below = [(0, 1 - colour)] + [(d, c) for d in range(1, width) for c in range(2)]
    above = [(d, c) for d in range(width - 1) for c in range(2)] + [(width - 1, 1 - colour)]
    if not first and width % 2 == 0:
        below.remove((width - 1, 0))
        above.remove((0, 0))
    return below, above


def kernel(n_rep, n_slab, source, spins_hbm, coup_hbm, out_hbm, spins, coup, out, raw, work, bonds, low, high, stage, land, res, c_send, c_recv, h_send, h_recv, r_send, r_recv, in_sem, out_sem):
    rep_dev, comps, planes, rows, cols = spins.shape
    pairs = rep_dev // 2
    width, half = WIDTH, rows // 2
    exchanges = 2 * SWEEPS // width
    group, slab = lax.axis_index("rep"), lax.axis_index("slab")
    up, down = lax.rem(slab + 1, n_slab), lax.rem(slab + n_slab - 1, n_slab)
    offsets = [(1 + j) % n_rep for j in range(pairs)]
    remote = [j for j in range(pairs) if offsets[j]]

    loads = [pltpu.make_async_copy(spins_hbm.at[pl.ds(2 * r, 2)], spins.at[pl.ds(2 * r, 2)], in_sem.at[r]) for r in range(pairs)]
    loads.append(pltpu.make_async_copy(coup_hbm, coup, in_sem.at[pairs]))
    for copy in loads:
        copy.start()

    barrier = pltpu.get_barrier_semaphore()
    for side in (up, down):
        pl.semaphore_signal(barrier, inc=1, device_id=(group, side), device_id_type=MESH)
    for j in remote:
        giver = lax.rem(group + offsets[j], n_rep)
        pl.semaphore_signal(barrier, inc=1, device_id=(giver, slab), device_id_type=MESH)
    def remote_copy(src, dst, send, recv, device):
        copy = pltpu.make_async_remote_copy(
            src_ref=src, dst_ref=dst, send_sem=send, recv_sem=recv, device_id=device, device_id_type=MESH
        )
        copy.start()
        return copy

    row = lax.broadcasted_iota(jnp.int32, (half, cols), 0)
    site = row + lax.broadcasted_iota(jnp.int32, (half, cols), 1)

    def front(plane):
        return ((site + (slab * planes + plane + width)) & 1) == 0

    def pack(mask, first, second):
        second = reverse_rows(second, row)
        return jnp.where(mask, first, second), jnp.where(mask, second, first)

    copies = {}

    def send_halo(r, e):
        colour = (e * width) % 2
        below, above = halo_items(width, colour, e == 0)
        for side, (items, start, device) in enumerate(((below, planes, up), (above, width, down))):
            for i, (d, c) in enumerate(items):
                for k in range(comps):
                    stage[e, side, r, i, k] = work[r, start + d, c, k]
            copies[r, e, side] = remote_copy(
                stage.at[e, side, r, pl.ds(0, len(items))],
                land.at[e, side, r, pl.ds(0, len(items))], h_send.at[e, side, r],
                h_recv.at[e, side, r],
                (group, device),
            )

    def take_halo(r, e):
        colour = (e * width) % 2
        below, above = halo_items(width, colour, e == 0)
        for side, (items, start) in enumerate(((below, 0), (above, planes + width))):
            copies[r, e, side].wait()
            for i, (d, c) in enumerate(items):
                for k in range(comps):
                    work[r, start + d, c, k] = land[e, side, r, i, k]

    kept = []
    for slot in range(rep_dev):
        own = group * rep_dev + slot
        kept.append(source[own] == own)

    for r in range(pairs):
        loads[r].wait()

        def pack_plane(p, carry, r=r):
            mask = front(p + width)
            for k in range(comps):
                value = jnp.where(kept[2 * r], spins[2 * r, k, p], spins[2 * r + 1, k, p])
                zero, one = pack(mask, value[:half], value[half:])
                work[r, p + width, 0, k] = zero
                work[r, p + width, 1, k] = one
                if r == 0 and remote:
                    raw[p, 0, k] = zero
                    raw[p, 1, k] = one
            return carry

        lax.fori_loop(0, planes, pack_plane, 0)

    def bonds_of(plane, jx, jy, jz, jz_below):
        mask = front(plane)
        jx, jy, jz, jz_below = [(2 * j - 1).astype(jnp.float32) for j in (jx, jy, jz, jz_below)]
        jw = pltpu.roll(jx, 1, 1)
        first, second = jy[:half], jy[half:]
        south_first = jnp.where(row == 0, second[half - 1 :], pltpu.roll(first, 1, 0))
        south_second = jnp.where(row == 0, first[half - 1 :], pltpu.roll(second, 1, 0))
        first_r = reverse_rows(second, row)
        south_r = reverse_rows(south_second, row)
        east = pack(mask, jx[:half], jx[half:])
        west = pack(mask, jw[:half], jw[half:])
        upper = pack(mask, jz[:half], jz[half:])
        lower = pack(mask, jz_below[:half], jz_below[half:])
        after = (jnp.where(mask, first, south_r), jnp.where(mask, south_r, first))
        before = (jnp.where(mask, south_first, first_r), jnp.where(mask, first_r, south_first))
        for i, bond in enumerate((east, west, after, before, upper, lower)):
            for c in range(2):
                bonds[plane, c, i] = bond[c]

    def own_bonds(p, carry):
        bonds_of(p + width, coup[0, p], coup[1, p], coup[2, p], coup[2, p - 1])
        return carry

    loads[pairs].wait()
    lax.fori_loop(1, planes, own_bonds, 0)
    pl.semaphore_wait(barrier, 2 + len(remote))

    bond_copies = [remote_copy(coup.at[2, planes - width], low.at[2, 0], c_send.at[0], c_recv.at[0], (group, up))]
    if width > 1:
        bond_copies.append(
            remote_copy(coup.at[:, planes - width + 1 : planes], low.at[:, 1:width], c_send.at[1], c_recv.at[1], (group, up))
        )
        bond_copies.append(remote_copy(coup.at[:, 0 : width - 1], high, c_send.at[2], c_recv.at[2], (group, down)))
    inner = pl.ds(width, planes)
    results, late = [], []
    for n, j in enumerate(remote):
        taker = lax.rem(group + n_rep - offsets[j], n_rep)
        late.append(remote_copy(raw, work.at[pairs + n, inner], r_send.at[n, 0], r_recv.at[n, 0], (taker, slab)))
    for r in range(pairs - 1, -1, -1):
        send_halo(r, 0)
    for copy in bond_copies:
        copy.wait()
    for p in range(1, width):
        bonds_of(p, low[0, p], low[1, p], low[2, p], low[2, p - 1])
    bonds_of(width, coup[0, 0], coup[1, 0], coup[2, 0], low[2, width - 1])
    for p in range(width - 1):
        beneath = coup[2, planes - 1] if p == 0 else high[2, p - 1]
        bonds_of(planes + width + p, high[0, p], high[1, p], high[2, p], beneath)

    def half_sweep(r, colour, first, last):
        other = 1 - colour

        def turned(p):
            east, west, after, before, upper, lower = [bonds[p, colour, i] for i in range(6)]
            field, spin = [], []
            for k in range(comps):
                q = work[r, p, other, k]
                north = jnp.where(row == half - 1, q, pltpu.roll(q, half - 1, 0))
                south = jnp.where(row == 0, q, pltpu.roll(q, 1, 0))
                h = east * pltpu.roll(q, cols - 1, 1) + west * pltpu.roll(q, 1, 1)
                h = h + after * north + before * south
                h = h + upper * work[r, p + 1, other, k] + lower * work[r, p - 1, other, k]
                field.append(h)
                spin.append(work[r, p, colour, k])
            along = sum(s * h for s, h in zip(spin, field))
            strength = sum(h * h for h in field)
            scale = 2.0 * along / jnp.maximum(strength, 1.0)
            return [scale * h - s for s, h in zip(spin, field)]

        count = last - first
        step = max(g for g in range(1, GROUP + 1) if count % g == 0)

        def some_planes(i, carry):
            base = first + i * step
            new = [turned(base + n) for n in range(step)]
            for n in range(step):
                for k in range(comps):
                    work[r, base + n, colour, k] = new[n][k]
            return carry

        lax.fori_loop(0, count // step, some_planes, 0)

    def advance(r, e):
        take_halo(r, e)
        for i in range(width):
            half_sweep(r, (e * width + i) % 2, i + 1, planes + 2 * width - 1 - i)
        if e < exchanges - 1:
            send_halo(r, e + 1)
        elif 1 <= r < pairs:
            for n, j in enumerate(remote):
                taker = lax.rem(group + n_rep - offsets[j], n_rep)
                results.append(
                    remote_copy(work.at[r, inner], res.at[n, r - 1], r_send.at[n, r], r_recv.at[n, r], (taker, slab))
                )

    for e in range(exchanges):
        for r in range(pairs - 1, -1, -1):
            advance(r, e)
        if e == 0:
            for n, copy in enumerate(late):
                copy.wait_recv()
                send_halo(pairs + n, 0)
        elif e < exchanges - 1:
            for n in range(len(late)):
                advance(pairs + n, e - 1)

    def write(j):
        if j in remote:
            n = remote.index(j)
            given = lambda r, p, c, k: res[n, r - 1, p, c, k] if r else work[pairs + n, p + width, c, k]
        else:
            given = lambda r, p, c, k: work[r, p + width, c, k]

        def write_plane(p, carry):
            mask = front(p + width)
            for slot in (2 * j, 2 * j + 1):
                pair = lax.rem(source[group * rep_dev + slot], rep_dev) // 2
                for k in range(comps):
                    colours = []
                    for c in range(2):
                        value = given(0, p, c, k)
                        for r in range(1, pairs):
                            value = jnp.where(pair == r, given(r, p, c, k), value)
                        colours.append(jnp.where(kept[slot], work[j, p + width, c, k], value))
                    zero, one = colours
                    out[slot, k, p, :half] = jnp.where(mask, zero, one)
                    out[slot, k, p, half:] = reverse_rows(jnp.where(mask, one, zero), row)
            return carry

        lax.fori_loop(0, planes, write_plane, 0)

    stores = []

    def store(j):
        write(j)
        stores.append(pltpu.make_async_copy(out.at[pl.ds(2 * j, 2)], out_hbm.at[pl.ds(2 * j, 2)], out_sem.at[j]))
        stores[-1].start()

    for j in range(pairs):
        if j not in remote:
            store(j)
    for e in range(max(exchanges - 2, 0), exchanges):
        for n in range(len(late)):
            advance(pairs + n, e)
    for copy in late:
        copy.wait_send()
    for copy in results:
        copy.wait()
    for j in remote:
        store(j)
    for copy in stores:
        copy.wait()


def solution(mesh):
    n_rep, n_slab = mesh.shape["rep"], mesh.shape["slab"]

    def local(spins, couplings, source):
        rep_dev, comps, planes, rows, cols = spins.shape
        pairs, half, width = rep_dev // 2, rows // 2, WIDTH
        exchanges, items = 2 * SWEEPS // width, 2 * width - 1
        n_remote = sum(1 for j in range(pairs) if (1 + j) % n_rep)
        deep = planes + 2 * width
        f32, i32, dma = jnp.float32, jnp.int32, pltpu.SemaphoreType.DMA
        return pl.pallas_call(
            functools.partial(kernel, n_rep, n_slab),
            out_shape=jax.ShapeDtypeStruct(spins.shape, f32),
            in_specs=[
                pl.BlockSpec(memory_space=pltpu.SMEM),
                pl.BlockSpec(memory_space=pl.ANY),
                pl.BlockSpec(memory_space=pl.ANY),
            ],
            out_specs=pl.BlockSpec(memory_space=pl.ANY),
            scratch_shapes=[
                pltpu.VMEM(spins.shape, f32),
                pltpu.VMEM(couplings.shape, i32),
                pltpu.VMEM(spins.shape, f32),
                pltpu.VMEM((planes, 2, comps, half, cols), f32),
                pltpu.VMEM((pairs + n_remote, deep, 2, comps, half, cols), f32),
                pltpu.VMEM((deep, 2, 6, half, cols), f32),
                pltpu.VMEM((3, width, rows, cols), i32),
                pltpu.VMEM((3, max(width - 1, 1), rows, cols), i32),
                pltpu.VMEM((exchanges, 2, pairs + n_remote, items, comps, half, cols), f32),
                pltpu.VMEM((exchanges, 2, pairs + n_remote, items, comps, half, cols), f32),
                pltpu.VMEM((max(n_remote, 1), pairs - 1, planes, 2, comps, half, cols), f32),
                dma((3,)),
                dma((3,)),
                dma((exchanges, 2, pairs + n_remote)),
                dma((exchanges, 2, pairs + n_remote)),
                dma((max(n_remote, 1), pairs)),
                dma((max(n_remote, 1), pairs)),
                dma((pairs + 1,)),
                dma((pairs,)),
            ],
            compiler_params=pltpu.CompilerParams(collective_id=0, has_side_effects=True),
        )(source, spins, couplings)

    in_specs = (P("rep", None, "slab", None, None), P(None, "slab", None, None), P())
    out_specs = P("rep", None, "slab", None, None)
    return jax.shard_map(local, mesh=mesh, in_specs=in_specs, out_specs=out_specs, check_vma=False)
```
